128 devices in a mesh: row: 8 (over y, core), col: 16 (over z, x).
Axes of the slice: x: 4, y: 4, z: 4, core: 2. Of those that a mesh axis runs over, the one named last changes fastest.
Arguments:
- tokens_in: bfloat16 [1024, 16384], P('row', 'col'), may hold values from -6 to 6
- out_grads: bfloat16 [1024, 16384], P('col', 'row'), may hold values from -0.1875 to 0.1875
- loc_rows: int32 [2048], replicated, may hold values from 0 to 16383
- loc_cols: int32 [2048], replicated, may hold values from 0 to 16383
Outputs:
- coef_grads: float32 [2048], P('col')
The draws below stay inside these ranges and needn't reach their ends.
All inputs are finite; a program needn't handle non-finite values.
Results may differ from the reference program's by a relative error of at most 0.0003.
Values may be sent and summed in bfloat16 or wider, within the bound.
A program may use at most 64 MiB of HBM per device.

```python
import math
import jax
import jax.numpy as jnp
from jax import lax

OUT = 16384
IN = 16384
TOKENS = 1024
LOCS = 2048


def set_ends(values, own_key, low, largest):
    shape = values.shape
    index_at = [jax.random.randint(jax.random.fold_in(own_key, axis), (), 0, shape[axis]) for axis in range(len(shape))]
    values = values.at[tuple(index_at)].set(low)
    longest = shape.index(max(shape))
    index_at[longest] = (index_at[longest] + 1) % shape[longest]
    return values.at[tuple(index_at)].set(largest)


def steps_of(rng, dims, pieces, least, high):
    factor_of = 1.0
    for dim, parts in pieces:
        draws = jax.random.uniform(jax.random.fold_in(jax.random.fold_in(rng, 6), dim), (parts,), jnp.float32, least / len(pieces), high / len(pieces))
        factor_of = factor_of * jnp.repeat(jnp.exp(draws), dims[dim] // parts).reshape((-1,) + (1,) * (len(dims) - 1 - dim))
    return factor_of


def scatter_about(stream_key, dims, width, reach, pieces=(), held_as=jnp.bfloat16):
    values = width * jax.random.normal(stream_key, dims, jnp.float32)
    if pieces:
        values = values * steps_of(stream_key, dims, pieces, -0.22, 0.18)
    return jnp.clip(values, -reach, reach).astype(held_as)


def setup_inputs(seed: int = 0) -> dict:
    arg_keys = jax.random.split(jax.random.key(seed), 5)
    tokens_in = scatter_about(arg_keys[0], (TOKENS, IN), 1.0, 6.0, ((0, 8), (1, 16)))
    out_grads = scatter_about(arg_keys[1], (TOKENS, OUT), 0.03125, 0.1875, ((0, 16), (1, 8)))
    loc_rows = set_ends(jax.random.randint(arg_keys[2], (LOCS,), 0, OUT), jax.random.fold_in(arg_keys[2], 1), 0, OUT - 1).astype(jnp.int32)
    loc_cols = set_ends(jax.random.randint(arg_keys[3], (LOCS,), 0, IN), jax.random.fold_in(arg_keys[3], 1), 0, IN - 1).astype(jnp.int32)
    return {"tokens_in": tokens_in, "out_grads": out_grads, "loc_rows": loc_rows, "loc_cols": loc_cols}


def cosine_table(frequency, first_row, row_count, length):
    position = first_row + jnp.arange(row_count).astype(jnp.int32)
    phase = (2 * position[None, :] + 1) * frequency.astype(jnp.int32)[:, None] % (4 * length)
    norming = jnp.where(frequency == 0, math.sqrt(1.0 / length), math.sqrt(2.0 / length))
    table = norming[:, None] * jnp.cos(phase.astype(jnp.float32) * (math.pi / (2 * length)))
    return table.astype(jnp.float32)

def reference(tokens_in, out_grads, loc_rows, loc_cols):
    locs = loc_rows.shape[0]
    block_size = math.gcd(locs, 256)
    pairs = (loc_rows.reshape(locs // block_size, block_size), loc_cols.reshape(locs // block_size, block_size))
    grads_wide = out_grads.astype(jnp.float32)
    inputs_wide = tokens_in.astype(jnp.float32)

    def one_block(pair):
        row_table = cosine_table(pair[0], 0, OUT, OUT)
        col_table = cosine_table(pair[1], 0, IN, IN)
        out_side = jnp.dot(grads_wide, row_table.T, precision=lax.Precision.HIGHEST, preferred_element_type=jnp.float32)
        in_side = jnp.dot(inputs_wide, col_table.T, precision=lax.Precision.HIGHEST, preferred_element_type=jnp.float32)
        return lax.optimization_barrier(jnp.sum(out_side * in_side, axis=0))
    return lax.map(one_block, pairs).reshape(-1)
```

```python
import math

import jax
import jax.numpy as jnp
import numpy as np
from jax import lax
from jax.experimental import pallas as pl
from jax.experimental.pallas import tpu as pltpu
from jax.sharding import PartitionSpec as P

N = 16384
HALF = 128
FP = 136
TOK = 8
MESH = pl.DeviceIdType.MESH
F32, BF16 = jnp.float32, jnp.bfloat16


def halves(table):
    high = table.astype(np.float32).astype(BF16)
    low = (table - high.astype(np.float64)).astype(np.float32).astype(BF16)
    return high, low


def tables():
    slot = np.arange(FP)[:, None]
    valid = (slot <= HALF).astype(np.float64)
    h = np.arange(HALF)[None, :]
    turn = 2 * np.pi * ((h * slot) % 256) / 256
    over_h = np.concatenate([np.cos(turn) * valid, np.sin(turn) * valid])
    high, low = halves(over_h)
    first = np.concatenate([high, low], axis=1)
    odd = 2 * h + 1
    turn = np.pi * (odd * slot) / (2 * N)
    twiddle = np.stack([np.cos(turn), np.sin(turn)]).astype(np.float32)
    g = np.concatenate([np.arange(64), np.arange(1, 65)])[None, :]
    sign = np.concatenate([-np.ones(64), np.ones(64)])[None, :]
    turn = np.pi * ((odd.T * g) % 256) / HALF
    over_l = np.concatenate([np.cos(turn), sign * np.sin(turn)])
    high, low = halves(over_l)
    second = np.concatenate([high, low], axis=1)
    return first, twiddle, second


def digits(loc):
    rest = loc & 255
    mirrored = rest > HALF
    slot = jnp.where(mirrored, 256 - rest, rest)
    column = (loc >> 8) + jnp.where(mirrored, 64, 0)
    return slot, column


def kernel(nr, nc, x_hbm, g_hbm, rows_hbm, cols_hbm, first_hbm, twiddle_hbm, second_hbm, o_ref,
           x_in, g_in, rows, cols, first, twiddle, second, spread, packed, z_high, z_low, d_pair,
           pick, picked, part, got_col, sent_row, got_row,
           local_sem, x_send, x_recv, g_send, g_recv, c_send, c_recv, r_send, r_recv):
    r, c = lax.axis_index("row"), lax.axis_index("col")
    locs = rows.shape[1]

    def x_dest(j):
        return lax.rem(j, nr), 2 * r + lax.div(j, nr)

    def is_me(row, col):
        return jnp.logical_and(row == r, col == c)

    barrier = pltpu.get_barrier_semaphore()

    def greet(row, col):
        pl.semaphore_signal(barrier, inc=1, device_id=(row, col), device_id_type=MESH)

    for i in range(1, nr):
        greet(lax.rem(r + i, nr), c)
    for i in range(1, nc):
        greet(r, lax.rem(c + i, nc))
    for i in range(nc):
        source = lax.rem(c + i, nc)

        @pl.when(jnp.logical_not(is_me(lax.div(c, 2), source)))
        def _():
            greet(lax.div(c, 2), source)

    loads = [(rows_hbm, rows), (cols_hbm, cols), (first_hbm, first), (twiddle_hbm, twiddle), (second_hbm, second)]
    loads = [pltpu.make_async_copy(a, b, local_sem.at[i]) for i, (a, b) in enumerate(loads)]
    for load in loads:
        load.start()

    kept = jnp.logical_and(c >= 2 * r, c < 2 * r + 2).astype(jnp.int32)
    pl.semaphore_wait(barrier, (nr - 1) + (nc - 1) + nc - kept)

    def g_copy(i):
        s = lax.rem(r + i, nr)
        return pltpu.make_async_remote_copy(
            src_ref=g_hbm.at[s], dst_ref=g_in.at[r], send_sem=g_send.at[i], recv_sem=g_recv.at[r],
            device_id=(s, c), device_id_type=MESH)

    def x_copy(i):
        j = lax.rem(c + i, nc)
        return pltpu.make_async_remote_copy(
            src_ref=x_hbm.at[j], dst_ref=x_in.at[c], send_sem=x_send.at[i], recv_sem=x_recv.at[c],
            device_id=x_dest(j), device_id_type=MESH)

    def x_stays(i):
        return is_me(*x_dest(lax.rem(c + i, nc)))

    def x_local(i):
        return pltpu.make_async_copy(x_hbm.at[lax.rem(c + i, nc)], x_in.at[c], x_recv.at[c])

    pltpu.make_async_copy(g_hbm.at[r], g_in.at[r], g_recv.at[r]).start()
    for i in range(1, nr):
        g_copy(i).start()
    for i in range(nc):
        @pl.when(x_stays(i))
        def _():
            x_local(i).start()

        @pl.when(jnp.logical_not(x_stays(i)))
        def _():
            x_copy(i).start()

    for load in loads:
        load.wait()

    for side, loc_ref in ((0, rows), (1, cols)):
        _, column = digits(loc_ref[...])
        lane = lax.broadcasted_iota(jnp.int32, (HALF, locs), 0)
        hot = (lane == column).astype(F32).astype(BF16)
        pick[side, :HALF, :] = hot
        pick[side, HALF:, :] = hot

    def spectrum(side, arrived, recv_sem, loc_ref):
        sources, _, width = arrived.shape
        steps = width // HALF
        for s in range(sources):
            pltpu.make_async_copy(arrived.at[s], arrived.at[s], recv_sem.at[s]).wait()
            block = arrived[s].astype(F32)
            for k in range(steps):
                spread[pl.ds((s * steps + k) * TOK, TOK), :] = block[:, k * HALF:(k + 1) * HALF]
        for t in range(TOK):
            column = spread[pl.ds(t, HALF, stride=TOK), :].astype(BF16)
            packed[:HALF, t * HALF:(t + 1) * HALF] = column
            packed[HALF:, t * HALF:(t + 1) * HALF] = column
        tc, ts = twiddle[0], twiddle[1]
        for t in range(TOK):
            if t % 2 == 0:
                both = jnp.dot(first[...], packed[:, t * HALF:(t + 2) * HALF], preferred_element_type=F32)
            y = both[:, (t % 2) * HALF:(t % 2 + 1) * HALF]
            yc, ys = y[:FP], y[FP:]
            for part_at, z in ((0, yc * tc - ys * ts), (HALF, yc * ts + ys * tc)):
                high = z.astype(BF16)
                z_high[t * FP:(t + 1) * FP, part_at:part_at + HALF] = high
                z_low[t * FP:(t + 1) * FP, part_at:part_at + HALF] = (z - high.astype(F32)).astype(BF16)
        wide = jnp.dot(z_high[...], second[...], preferred_element_type=F32)
        d = wide[:, :HALF] + wide[:, HALF:] + jnp.dot(z_low[...], second[:, :HALF], preferred_element_type=F32)
        high = d.astype(BF16)
        d_pair[:, :HALF] = high
        d_pair[:, HALF:] = (d - high.astype(F32)).astype(BF16)
        tile = 256
        for k in range(locs // tile):
            at = slice(k * tile, (k + 1) * tile)
            slot, _ = digits(loc_ref[:, at])
            found = jnp.dot(d_pair[...], pick[side, :, at], preferred_element_type=F32)
            mask = lax.broadcasted_iota(jnp.int32, (FP, tile), 0) == slot
            for t in range(TOK):
                mine = jnp.where(mask, found[t * FP:(t + 1) * FP], 0.0)
                picked[side, t:t + 1, at] = jnp.sum(mine, axis=0, keepdims=True)

    spectrum(0, g_in, g_recv, rows)
    spectrum(1, x_in, x_recv, cols)

    def norming(loc_ref):
        return jnp.where(loc_ref[...] == 0, math.sqrt(1.0 / N), math.sqrt(2.0 / N))

    total = jnp.sum(picked[0] * picked[1], axis=0, keepdims=True) * (norming(rows) * norming(cols))
    width = locs // nc
    for k in range(nc):
        part[k] = total[:, k * width:(k + 1) * width]

    got_col[c] = part[c]

    def col_copy(i):
        d = lax.rem(c + i, nc)
        return pltpu.make_async_remote_copy(
            src_ref=part.at[d], dst_ref=got_col.at[c], send_sem=c_send.at[i], recv_sem=c_recv.at[c],
            device_id=(r, d), device_id_type=MESH)

    for i in range(1, nc):
        col_copy(i).start()
    for i in range(1, nc):
        d = lax.rem(c + i, nc)
        pltpu.make_async_copy(got_col.at[d], got_col.at[d], c_recv.at[d]).wait()
    mine = got_col[0]
    for k in range(1, nc):
        mine = mine + got_col[k]
    sent_row[...] = mine
    got_row[r] = mine

    def row_copy(i):
        d = lax.rem(r + i, nr)
        return pltpu.make_async_remote_copy(
            src_ref=sent_row, dst_ref=got_row.at[r], send_sem=r_send.at[i], recv_sem=r_recv.at[r],
            device_id=(d, c), device_id_type=MESH)

    for i in range(1, nr):
        row_copy(i).start()
    for i in range(1, nr):
        d = lax.rem(r + i, nr)
        pltpu.make_async_copy(got_row.at[d], got_row.at[d], r_recv.at[d]).wait()
    result = got_row[0]
    for k in range(1, nr):
        result = result + got_row[k]
    o_ref[...] = result

    for i in range(1, nr):
        g_copy(i).wait_send()
        row_copy(i).wait_send()
    for i in range(1, nc):
        col_copy(i).wait_send()
    for i in range(nc):
        @pl.when(jnp.logical_not(x_stays(i)))
        def _():
            x_copy(i).wait_send()


def solution(mesh):
    nr, nc = mesh.shape["row"], mesh.shape["col"]
    first, twiddle, second = tables()

    def local(tokens_in, out_grads, loc_rows, loc_cols):
        locs = loc_rows.shape[0]
        x = tokens_in.reshape(nc, TOK, tokens_in.shape[1])
        g = out_grads.reshape(nr, TOK, out_grads.shape[1])
        width = locs // nc
        dma = pltpu.SemaphoreType.DMA
        out = pl.pallas_call(
            lambda *refs: kernel(nr, nc, *refs),
            out_shape=jax.ShapeDtypeStruct((1, width), F32),
            in_specs=[pl.BlockSpec(memory_space=pl.ANY)] * 7,
            out_specs=pl.BlockSpec(memory_space=pltpu.VMEM),
            scratch_shapes=[
                pltpu.VMEM((nc, TOK, x.shape[2]), BF16),
                pltpu.VMEM((nr, TOK, g.shape[2]), BF16),
                pltpu.VMEM((1, locs), jnp.int32),
                pltpu.VMEM((1, locs), jnp.int32),
                pltpu.VMEM(first.shape, BF16),
                pltpu.VMEM(twiddle.shape, F32),
                pltpu.VMEM(second.shape, BF16),
                pltpu.VMEM((HALF * TOK, HALF), F32),
                pltpu.VMEM((2 * HALF, TOK * HALF), BF16),
                pltpu.VMEM((TOK * FP, 2 * HALF), BF16),
                pltpu.VMEM((TOK * FP, 2 * HALF), BF16),
                pltpu.VMEM((TOK * FP, 2 * HALF), BF16),
                pltpu.VMEM((2, 2 * HALF, locs), BF16),
                pltpu.VMEM((2, TOK, locs), F32),
                pltpu.VMEM((nc, 1, width), F32),
                pltpu.VMEM((nc, 1, width), F32),
                pltpu.VMEM((1, width), F32),
                pltpu.VMEM((nr, 1, width), F32),
                dma((5,)), dma((nc,)), dma((nc,)), dma((nr,)), dma((nr,)),
                dma((nc,)), dma((nc,)), dma((nr,)), dma((nr,)),
            ],
            compiler_params=pltpu.CompilerParams(collective_id=0, has_side_effects=True, vmem_limit_bytes=48 << 20),
            name="spectral",
        )(x, g, loc_rows.reshape(1, locs), loc_cols.reshape(1, locs),
          jnp.asarray(first), jnp.asarray(twiddle), jnp.asarray(second))
        return out.reshape(width)

    in_specs = (P("row", "col"), P("col", "row"), P(), P())
    return jax.shard_map(local, mesh=mesh, in_specs=in_specs, out_specs=P("col"), check_vma=False)
```

```python
import math

import jax
import jax.numpy as jnp
import numpy as np
from jax import lax
from jax.experimental import pallas as pl
from jax.experimental.pallas import tpu as pltpu
from jax.sharding import PartitionSpec as P

N = 16384
HALF = 128
FP = 136
TOK = 8
MESH = pl.DeviceIdType.MESH
F32, BF16 = jnp.float32, jnp.bfloat16


def halves(table):
    high = table.astype(np.float32).astype(BF16)
    low = (table - high.astype(np.float64)).astype(np.float32).astype(BF16)
    return high, low


def tables():
    slot = np.arange(FP)[:, None]
    valid = (slot <= HALF).astype(np.float64)
    h = np.arange(HALF)[None, :]
    turn = 2 * np.pi * ((h * slot) % 256) / 256
    over_h = np.concatenate([np.cos(turn) * valid, np.sin(turn) * valid])
    high, low = halves(over_h)
    first = np.concatenate([high, low], axis=1)
    odd = 2 * h + 1
    turn = np.pi * (odd * slot) / (2 * N)
    twiddle = np.stack([np.cos(turn), np.sin(turn)]).astype(np.float32)
    g = np.concatenate([np.arange(64), np.arange(1, 65)])[None, :]
    sign = np.concatenate([-np.ones(64), np.ones(64)])[None, :]
    turn = np.pi * ((odd.T * g) % 256) / HALF
    over_l = np.concatenate([np.cos(turn), sign * np.sin(turn)])
    high, low = halves(over_l)
    second = np.concatenate([high, low], axis=1)
    return first, twiddle, second


def digits(loc):
    rest = loc & 255
    mirrored = rest > HALF
    slot = jnp.where(mirrored, 256 - rest, rest)
    column = (loc >> 8) + jnp.where(mirrored, 64, 0)
    return slot, column


def kernel(nr, nc, x_hbm, g_hbm, rows_hbm, cols_hbm, first_hbm, twiddle_hbm, second_hbm, o_ref,
           x_in, g_in, rows, cols, first, twiddle, second, spread, packed, z_high, z_low, d_pair,
           pick, picked, part, got,
           load_sem, x_send, x_recv, g_send, g_recv, p_send, p_recv, x_ready, g_ready, peers, everyone):
    r, c = lax.axis_index("row"), lax.axis_index("col")
    y, core, z, x = r // 2, r % 2, c // 4, c % 4
    locs = rows.shape[1]

    def row_place(row):
        return (4 * (row // 2) - 2 * (row % 2)) * nr * nc + row

    def col_place(col):
        return (6 * (col // 4) + 5 * (col % 4) - 7 * (col % 4 // 3)) * nr * nc + col * nr

    def place_of(device):
        return row_place(device[0]) + col_place(device[1])

    place = place_of((r, c))

    x_row = 2 * z + x // 2
    my_g = 2 * ((y - z + 4) % 4) + core
    my_x = nr * (x % 2) + my_g

    def x_dest(j):
        return 2 * ((y + j // 2) % 4) + j % 2, 4 * y + 2 * core + j // nr

    def g_dest(s):
        return 2 * ((z + s // 2) % 4) + s % 2, c

    def signal(sem, device):
        pl.semaphore_signal(sem, inc=1, device_id=device, device_id_type=MESH)

    barrier = pltpu.get_barrier_semaphore()
    partners = [x_dest(j) for j in range(nc)] + [(x_row, j) for j in range(nc)] + [(r, j) for j in range(nc)]
    partners += [(s, c) for s in range(nr)]
    count = 0
    for device in partners:
        there = place_of(device)

        @pl.when(there > place)
        def _():
            signal(barrier, device)

        count = count + (there < place).astype(jnp.int32)

    loads = [(rows_hbm, rows), (cols_hbm, cols), (first_hbm, first), (twiddle_hbm, twiddle), (second_hbm, second)]
    loads = [pltpu.make_async_copy(a, b, load_sem.at[i]) for i, (a, b) in enumerate(loads)]
    for load in loads:
        load.start()

    def wait_for(sem, number):
        @pl.when(number > 0)
        def _():
            pl.semaphore_wait(sem, number)

    wait_for(barrier, count)

    def tell_earlier(sem, device):
        @pl.when(place_of(device) < place)
        def _():
            signal(sem, device)

    def g_copy(i):
        s = (r + i) % nr
        return s, g_dest(s), g_hbm.at[s], g_in.at[r], g_send, g_recv.at[y]

    def x_copy(i):
        j = (c + i) % nc
        return j, x_dest(j), x_hbm.at[j], x_in.at[c], x_send, x_recv.at[z]

    def remote(device, src, dst, send_sem, recv_sem):
        return pltpu.make_async_remote_copy(
            src_ref=src, dst_ref=dst, send_sem=send_sem, recv_sem=recv_sem,
            device_id=device, device_id_type=MESH)

    def send_early(copy):
        _, device, src, dst, _, recv_sem = copy

        @pl.when(place_of(device) < place)
        def _():
            remote(*copy[1:]).start()

        @pl.when(place_of(device) == place)
        def _():
            pltpu.make_async_copy(src, dst, recv_sem).start()

    def send_late(copy, ready):
        group, device = copy[:2]

        @pl.when(place_of(device) > place)
        def _():
            pl.semaphore_wait(ready.at[group], 1)
            remote(*copy[1:]).start()

    for s in range(nr):
        tell_earlier(g_ready.at[my_g], (s, c))
    for j in range(nc):
        tell_earlier(x_ready.at[my_x], (x_row, j))
    for i in range(nr):
        send_early(g_copy(i))
    for i in range(nc):
        send_early(x_copy(i))
    for j in range(nc):
        tell_earlier(peers, (r, j))
    for i in range(nr):
        send_late(g_copy(i), g_ready)
    for i in range(nc):
        send_late(x_copy(i), x_ready)

    for load in loads:
        load.wait()

    for side, loc_ref in ((0, rows), (1, cols)):
        _, column = digits(loc_ref[...])
        lane = lax.broadcasted_iota(jnp.int32, (HALF, locs), 0)
        hot = (lane == column).astype(F32).astype(BF16)
        pick[side, :HALF, :] = hot
        pick[side, HALF:, :] = hot

    def spectrum(side, arrived, recv_sem, loc_ref):
        sources, _, width = arrived.shape
        steps = width // HALF
        for s in range(sources):
            if s % (sources // 4) == 0:
                some = arrived.at[pl.ds(s, sources // 4)]
                pltpu.make_async_copy(some, some, recv_sem.at[4 * s // sources]).wait()
            block = arrived[s].astype(F32)
            for k in range(steps):
                spread[pl.ds((s * steps + k) * TOK, TOK), :] = block[:, k * HALF:(k + 1) * HALF]
        for t in range(TOK):
            column = spread[pl.ds(t, HALF, stride=TOK), :].astype(BF16)
            packed[:HALF, t * HALF:(t + 1) * HALF] = column
            packed[HALF:, t * HALF:(t + 1) * HALF] = column
        tc, ts = twiddle[0], twiddle[1]
        for t in range(TOK):
            if t % 2 == 0:
                both = jnp.dot(first[...], packed[:, t * HALF:(t + 2) * HALF], preferred_element_type=F32)
            y = both[:, (t % 2) * HALF:(t % 2 + 1) * HALF]
            yc, ys = y[:FP], y[FP:]
            for part_at, z in ((0, yc * tc - ys * ts), (HALF, yc * ts + ys * tc)):
                high = z.astype(BF16)
                z_high[t * FP:(t + 1) * FP, part_at:part_at + HALF] = high
                z_low[t * FP:(t + 1) * FP, part_at:part_at + HALF] = (z - high.astype(F32)).astype(BF16)
        wide = jnp.dot(z_high[...], second[...], preferred_element_type=F32)
        d = wide[:, :HALF] + wide[:, HALF:] + jnp.dot(z_low[...], second[:, :HALF], preferred_element_type=F32)
        high = d.astype(BF16)
        d_pair[:, :HALF] = high
        d_pair[:, HALF:] = (d - high.astype(F32)).astype(BF16)
        tile = 256
        for k in range(locs // tile):
            at = slice(k * tile, (k + 1) * tile)
            slot, _ = digits(loc_ref[:, at])
            found = jnp.dot(d_pair[...], pick[side, :, at], preferred_element_type=F32)
            mask = lax.broadcasted_iota(jnp.int32, (FP, tile), 0) == slot
            for t in range(TOK):
                mine = jnp.where(mask, found[t * FP:(t + 1) * FP], 0.0)
                picked[side, t:t + 1, at] = jnp.sum(mine, axis=0, keepdims=True)

    wait_for(peers, sum((place_of((r, j)) > place).astype(jnp.int32) for j in range(nc)))
    for i in range(1, nr):
        signal(everyone, ((r + i) % nr, c))

    spectrum(0, g_in, g_recv, rows)

    spectrum(1, x_in, x_recv, cols)

    def norming(loc_ref):
        return jnp.where(loc_ref[...] == 0, math.sqrt(1.0 / N), math.sqrt(2.0 / N))

    total = jnp.sum(picked[0] * picked[1], axis=0, keepdims=True) * (norming(rows) * norming(cols))
    width = locs // nc
    for k in range(nc):
        part[k] = total[:, k * width:(k + 1) * width]

    pl.semaphore_wait(everyone, nr - 1)
    mine = c + nc * r
    pltpu.make_async_copy(part.at[c], got.at[mine], p_recv).start()
    for i in range(nr):
        for k in range(nc):
            if i + k:
                row, col = (r + i) % nr, (c + k) % nc
                remote((row, col), part.at[col], got.at[mine], p_send, p_recv).start()
    pltpu.make_async_copy(got, got, p_recv).wait()
    o_ref[...] = jnp.sum(got[...], axis=0)

    sent = got.at[pl.ds(0, nr * nc - 1)]
    pltpu.make_async_copy(sent, sent, p_send).wait()

    def all_sent(copies, source, sem):
        n = source.shape[0]
        stays = [(place_of(device) == place).astype(jnp.int32) for _, device, *_ in copies]
        stays = sum(stays[1:], stays[0])
        for left in (0, 1):
            @pl.when(stays == left)
            def _():
                moved = source.at[pl.ds(0, n - left)]
                pltpu.make_async_copy(moved, moved, sem).wait()

    all_sent([g_copy(i) for i in range(nr)], g_hbm, g_send)
    all_sent([x_copy(i) for i in range(nc)], x_hbm, x_send)


def solution(mesh):
    nr, nc = mesh.shape["row"], mesh.shape["col"]
    first, twiddle, second = tables()

    def local(tokens_in, out_grads, loc_rows, loc_cols):
        locs = loc_rows.shape[0]
        x = tokens_in.reshape(nc, TOK, tokens_in.shape[1])
        g = out_grads.reshape(nr, TOK, out_grads.shape[1])
        width = locs // nc
        dma, regular = pltpu.SemaphoreType.DMA, pltpu.SemaphoreType.REGULAR
        out = pl.pallas_call(
            lambda *refs: kernel(nr, nc, *refs),
            out_shape=jax.ShapeDtypeStruct((1, width), F32),
            in_specs=[pl.BlockSpec(memory_space=pl.ANY)] * 7,
            out_specs=pl.BlockSpec(memory_space=pltpu.VMEM),
            scratch_shapes=[
                pltpu.VMEM((nc, TOK, x.shape[2]), BF16),
                pltpu.VMEM((nr, TOK, g.shape[2]), BF16),
                pltpu.VMEM((1, locs), jnp.int32),
                pltpu.VMEM((1, locs), jnp.int32),
                pltpu.VMEM(first.shape, BF16),
                pltpu.VMEM(twiddle.shape, F32),
                pltpu.VMEM(second.shape, BF16),
                pltpu.VMEM((HALF * TOK, HALF), F32),
                pltpu.VMEM((2 * HALF, TOK * HALF), BF16),
                pltpu.VMEM((TOK * FP, 2 * HALF), BF16),
                pltpu.VMEM((TOK * FP, 2 * HALF), BF16),
                pltpu.VMEM((TOK * FP, 2 * HALF), BF16),
                pltpu.VMEM((2, 2 * HALF, locs), BF16),
                pltpu.VMEM((2, TOK, locs), F32),
                pltpu.VMEM((nc, 1, width), F32),
                pltpu.VMEM((nr * nc, 1, width), F32),
                dma((5,)), dma, dma((4,)), dma, dma((4,)), dma, dma,
                regular((nc,)), regular((nr,)), regular, regular,
            ],
            compiler_params=pltpu.CompilerParams(collective_id=0, has_side_effects=True),
            name="spectral",
        )(x, g, loc_rows.reshape(1, locs), loc_cols.reshape(1, locs),
          jnp.asarray(first), jnp.asarray(twiddle), jnp.asarray(second))
        return out.reshape(width)

    in_specs = (P("row", "col"), P("col", "row"), P(), P())
    return jax.shard_map(local, mesh=mesh, in_specs=in_specs, out_specs=P("col"), check_vma=False)
```

```python
import math

import jax
import jax.numpy as jnp
import numpy as np
from jax import lax
from jax.experimental import pallas as pl
from jax.experimental.pallas import tpu as pltpu
from jax.sharding import PartitionSpec as P

N = 16384
HALF = 128
FP = 136
TOK = 8
MESH = pl.DeviceIdType.MESH
F32, BF16 = jnp.float32, jnp.bfloat16


def halves(table):
    high = table.astype(np.float32).astype(BF16)
    low = (table - high.astype(np.float64)).astype(np.float32).astype(BF16)
    return high, low


def tables():
    slot = np.arange(FP)[:, None]
    valid = (slot <= HALF).astype(np.float64)
    h = np.arange(HALF)[None, :]
    turn = 2 * np.pi * ((h * slot) % 256) / 256
    over_h = np.concatenate([np.cos(turn) * valid, np.sin(turn) * valid])
    high, low = halves(over_h)
    first = np.concatenate([high, low], axis=1)
    odd = 2 * h + 1
    turn = np.pi * (odd * slot) / (2 * N)
    twiddle = np.stack([np.cos(turn), np.sin(turn)]).astype(np.float32)
    g = np.concatenate([np.arange(64), np.arange(1, 65)])[None, :]
    sign = np.concatenate([-np.ones(64), np.ones(64)])[None, :]
    turn = np.pi * ((odd.T * g) % 256) / HALF
    over_l = np.concatenate([np.cos(turn), sign * np.sin(turn)])
    high, low = halves(over_l)
    second = np.concatenate([high, low], axis=1)
    return first, twiddle, second


def digits(loc):
    rest = loc & 255
    mirrored = rest > HALF
    slot = jnp.where(mirrored, 256 - rest, rest)
    column = (loc >> 8) + jnp.where(mirrored, 64, 0)
    return slot, column


def kernel(nr, nc, x_hbm, g_hbm, rows_hbm, cols_hbm, first_hbm, twiddle_hbm, second_hbm, o_ref,
           x_own, g_own, x_in, g_in, rows, cols, first, twiddle, second, spread, packed, z_high, z_low, d_pair,
           pick, picked, part, got,
           load_sem, own_sem, x_send, x_recv, g_send, g_recv, p_send, p_recv, x_ready, g_ready, peers, everyone):
    r, c = lax.axis_index("row"), lax.axis_index("col")
    y, core, z, x = r >> 1, r & 1, c >> 2, c & 3
    locs = rows.shape[1]

    own = [pltpu.make_async_copy(g_hbm, g_own, own_sem.at[0]), pltpu.make_async_copy(x_hbm, x_own, own_sem.at[1])]
    for load in own:
        load.start()

    def row_place(row):
        at = row >> 1
        return (8 * ((at + 3) >> 2) - ((at + 1) >> 2) - 3 * (row & 1)) * nr * nc + row

    def col_place(col):
        plane, at = col >> 2, col & 3
        late = 9 * ((plane + 3) >> 2) + 3 * (plane >> 1) + ((plane + 1) >> 2) + at + ((at + 1) >> 2)
        return late * nr * nc + col * nr

    def place_of(device):
        return row_place(device[0]) + col_place(device[1])

    place = place_of((r, c))

    x_row = 2 * z + (x >> 1)
    my_g = 2 * ((y - z + 4) & 3) + core
    my_x = nr * (x & 1) + my_g

    def x_dest(j):
        return 2 * ((y + (j >> 1)) & 3) + (j & 1), 4 * y + 2 * core + (j >> 3)

    def g_dest(s):
        return 2 * ((z + (s >> 1)) & 3) + (s & 1), c

    def signal(sem, device):
        pl.semaphore_signal(sem, inc=1, device_id=device, device_id_type=MESH)

    barrier = pltpu.get_barrier_semaphore()
    partners = [x_dest(j) for j in range(nc)] + [(x_row, j) for j in range(nc)] + [(r, j) for j in range(nc)]
    partners += [(s, c) for s in range(nr)]
    count = 0
    for device in partners:
        there = place_of(device)

        @pl.when(there > place)
        def _():
            signal(barrier, device)

        count = count + (there < place).astype(jnp.int32)

    loads = [(rows_hbm, rows), (cols_hbm, cols), (first_hbm, first), (twiddle_hbm, twiddle), (second_hbm, second)]
    loads = [pltpu.make_async_copy(a, b, load_sem.at[i]) for i, (a, b) in enumerate(loads)]
    for load in loads:
        load.start()

    def wait_for(sem, number):
        @pl.when(number > 0)
        def _():
            pl.semaphore_wait(sem, number)

    wait_for(barrier, count)

    def tell_earlier(sem, device):
        @pl.when(place_of(device) < place)
        def _():
            signal(sem, device)

    def g_copy(i):
        s = (r + i) & (nr - 1)
        return s, g_dest(s), g_own.at[s], g_in.at[r], g_send, g_recv.at[y]

    def x_copy(i):
        j = (c + i) & (nc - 1)
        return j, x_dest(j), x_own.at[j], x_in.at[c], x_send, x_recv.at[z]

    def remote(device, src, dst, send_sem, recv_sem):
        return pltpu.make_async_remote_copy(
            src_ref=src, dst_ref=dst, send_sem=send_sem, recv_sem=recv_sem,
            device_id=device, device_id_type=MESH)

    def send_early(copy):
        _, device, src, dst, _, recv_sem = copy

        @pl.when(place_of(device) < place)
        def _():
            remote(*copy[1:]).start()

        @pl.when(place_of(device) == place)
        def _():
            pltpu.make_async_copy(src, dst, recv_sem).start()

    def send_late(copy, ready):
        group, device = copy[:2]

        @pl.when(place_of(device) > place)
        def _():
            pl.semaphore_wait(ready.at[group], 1)
            remote(*copy[1:]).start()

    for s in range(nr):
        tell_earlier(g_ready.at[my_g], (s, c))
    for j in range(nc):
        tell_earlier(x_ready.at[my_x], (x_row, j))
    own[0].wait()
    for i in range(nr):
        send_early(g_copy(i))
    own[1].wait()
    for i in range(nc):
        send_early(x_copy(i))
    for j in range(nc):
        tell_earlier(peers, (r, j))
    for i in range(nr):
        send_late(g_copy(i), g_ready)
    for i in range(nc):
        send_late(x_copy(i), x_ready)

    for load in loads:
        load.wait()

    for side, loc_ref in ((0, rows), (1, cols)):
        _, column = digits(loc_ref[...])
        lane = lax.broadcasted_iota(jnp.int32, (HALF, locs), 0)
        hot = (lane == column).astype(F32).astype(BF16)
        pick[side, :HALF, :] = hot
        pick[side, HALF:, :] = hot

    def spectrum(side, arrived, recv_sem, loc_ref):
        sources, _, width = arrived.shape
        steps = width // HALF
        for s in range(sources):
            if s % (sources // 4) == 0:
                some = arrived.at[pl.ds(s, sources // 4)]
                pltpu.make_async_copy(some, some, recv_sem.at[4 * s // sources]).wait()
            block = arrived[s].astype(F32)
            for k in range(steps):
                spread[pl.ds((s * steps + k) * TOK, TOK), :] = block[:, k * HALF:(k + 1) * HALF]
        for t in range(TOK):
            column = spread[pl.ds(t, HALF, stride=TOK), :].astype(BF16)
            packed[:HALF, t * HALF:(t + 1) * HALF] = column
            packed[HALF:, t * HALF:(t + 1) * HALF] = column
        tc, ts = twiddle[0], twiddle[1]
        for t in range(TOK):
            if t % 2 == 0:
                both = jnp.dot(first[...], packed[:, t * HALF:(t + 2) * HALF], preferred_element_type=F32)
            y = both[:, (t % 2) * HALF:(t % 2 + 1) * HALF]
            yc, ys = y[:FP], y[FP:]
            for part_at, z in ((0, yc * tc - ys * ts), (HALF, yc * ts + ys * tc)):
                high = z.astype(BF16)
                z_high[t * FP:(t + 1) * FP, part_at:part_at + HALF] = high
                z_low[t * FP:(t + 1) * FP, part_at:part_at + HALF] = (z - high.astype(F32)).astype(BF16)
        wide = jnp.dot(z_high[...], second[...], preferred_element_type=F32)
        d = wide[:, :HALF] + wide[:, HALF:] + jnp.dot(z_low[...], second[:, :HALF], preferred_element_type=F32)
        high = d.astype(BF16)
        d_pair[:, :HALF] = high
        d_pair[:, HALF:] = (d - high.astype(F32)).astype(BF16)
        tile, group = 256, TOK // 2
        for k in range(locs // tile):
            at = slice(k * tile, (k + 1) * tile)
            slot, _ = digits(loc_ref[:, at])
            mask = lax.broadcasted_iota(jnp.int32, (FP, tile), 0) == slot
            for start in range(0, TOK, group):
                lines = d_pair[start * FP:(start + group) * FP, :]
                found = jnp.dot(lines, pick[side, :, at], preferred_element_type=F32)
                for t in range(group):
                    mine = jnp.where(mask, found[t * FP:(t + 1) * FP], 0.0)
                    picked[side, start + t:start + t + 1, at] = jnp.sum(mine, axis=0, keepdims=True)

    wait_for(peers, sum((place_of((r, j)) > place).astype(jnp.int32) for j in range(nc)))
    for i in range(1, nr):
        signal(everyone, ((r + i) & (nr - 1), c))

    spectrum(0, g_in, g_recv, rows)

    spectrum(1, x_in, x_recv, cols)

    def norming(loc_ref):
        return jnp.where(loc_ref[...] == 0, math.sqrt(1.0 / N), math.sqrt(2.0 / N))

    total = jnp.sum(picked[0] * picked[1], axis=0, keepdims=True) * (norming(rows) * norming(cols))
    width = locs // nc
    for k in range(nc):
        part[k] = total[:, k * width:(k + 1) * width]

    pl.semaphore_wait(everyone, nr - 1)
    mine = c + nc * r
    pltpu.make_async_copy(part.at[c], got.at[mine], p_recv).start()
    for i in range(nr):
        for k in range(nc):
            if i + k:
                row, col = (r + i) & (nr - 1), (c + k) & (nc - 1)
                remote((row, col), part.at[col], got.at[mine], p_send, p_recv).start()
    pltpu.make_async_copy(got, got, p_recv).wait()
    o_ref[...] = jnp.sum(got[...], axis=0)

    sent = got.at[pl.ds(0, nr * nc - 1)]
    pltpu.make_async_copy(sent, sent, p_send).wait()

    def all_sent(copies, source, sem):
        n = source.shape[0]
        stays = [(place_of(device) == place).astype(jnp.int32) for _, device, *_ in copies]
        stays = sum(stays[1:], stays[0])
        for left in (0, 1):
            @pl.when(stays == left)
            def _():
                moved = source.at[pl.ds(0, n - left)]
                pltpu.make_async_copy(moved, moved, sem).wait()

    all_sent([g_copy(i) for i in range(nr)], g_own, g_send)
    all_sent([x_copy(i) for i in range(nc)], x_own, x_send)


def solution(mesh):
    nr, nc = mesh.shape["row"], mesh.shape["col"]
    first, twiddle, second = tables()

    def local(tokens_in, out_grads, loc_rows, loc_cols):
        locs = loc_rows.shape[0]
        x = tokens_in.reshape(nc, TOK, tokens_in.shape[1])
        g = out_grads.reshape(nr, TOK, out_grads.shape[1])
        width = locs // nc
        dma, regular = pltpu.SemaphoreType.DMA, pltpu.SemaphoreType.REGULAR
        out = pl.pallas_call(
            lambda *refs: kernel(nr, nc, *refs),
            out_shape=jax.ShapeDtypeStruct((1, width), F32),
            in_specs=[pl.BlockSpec(memory_space=pl.ANY)] * 7,
            out_specs=pl.BlockSpec(memory_space=pltpu.VMEM),
            scratch_shapes=[
                pltpu.VMEM(x.shape, BF16),
                pltpu.VMEM(g.shape, BF16),
                pltpu.VMEM((nc, TOK, x.shape[2]), BF16),
                pltpu.VMEM((nr, TOK, g.shape[2]), BF16),
                pltpu.VMEM((1, locs), jnp.int32),
                pltpu.VMEM((1, locs), jnp.int32),
                pltpu.VMEM(first.shape, BF16),
                pltpu.VMEM(twiddle.shape, F32),
                pltpu.VMEM(second.shape, BF16),
                pltpu.VMEM((HALF * TOK, HALF), F32),
                pltpu.VMEM((2 * HALF, TOK * HALF), BF16),
                pltpu.VMEM((TOK * FP, 2 * HALF), BF16),
                pltpu.VMEM((TOK * FP, 2 * HALF), BF16),
                pltpu.VMEM((TOK * FP, 2 * HALF), BF16),
                pltpu.VMEM((2, 2 * HALF, locs), BF16),
                pltpu.VMEM((2, TOK, locs), F32),
                pltpu.VMEM((nc, 1, width), F32),
                pltpu.VMEM((nr * nc, 1, width), F32),
                dma((5,)), dma((2,)), dma, dma((4,)), dma, dma((4,)), dma, dma,
                regular((nc,)), regular((nr,)), regular, regular,
            ],
            compiler_params=pltpu.CompilerParams(collective_id=0, has_side_effects=True),
            name="spectral",
        )(x, g, loc_rows.reshape(1, locs), loc_cols.reshape(1, locs),
          jnp.asarray(first), jnp.asarray(twiddle), jnp.asarray(second))
        return out.reshape(width)

    in_specs = (P("row", "col"), P("col", "row"), P(), P())
    return jax.shard_map(local, mesh=mesh, in_specs=in_specs, out_specs=P("col"), check_vma=False)
```

```python
import math

import jax
import jax.numpy as jnp
import numpy as np
from jax import lax
from jax.experimental import pallas as pl
from jax.experimental.pallas import tpu as pltpu
from jax.sharding import PartitionSpec as P

N = 16384
HALF = 128
FP = 136
TOK = 8
MESH = pl.DeviceIdType.MESH
F32, BF16 = jnp.float32, jnp.bfloat16


def halves(table):
    high = table.astype(np.float32).astype(BF16)
    low = (table - high.astype(np.float64)).astype(np.float32).astype(BF16)
    return high, low


def tables():
    slot = np.arange(FP)[:, None]
    valid = (slot <= HALF).astype(np.float64)
    h = np.arange(HALF)[None, :]
    turn = 2 * np.pi * ((h * slot) % 256) / 256
    over_h = np.concatenate([np.cos(turn) * valid, np.sin(turn) * valid])
    high, low = halves(over_h)
    first = np.concatenate([high, low], axis=1)
    odd = 2 * h + 1
    turn = np.pi * (odd * slot) / (2 * N)
    twiddle = np.stack([np.cos(turn), np.sin(turn)]).astype(np.float32)
    g = np.concatenate([np.arange(64), np.arange(1, 65)])[None, :]
    sign = np.concatenate([-np.ones(64), np.ones(64)])[None, :]
    turn = np.pi * ((odd.T * g) % 256) / HALF
    over_l = np.concatenate([np.cos(turn), sign * np.sin(turn)])
    high, low = halves(over_l)
    second = np.concatenate([high, low], axis=1)
    return first, twiddle, second


def digits(loc):
    rest = loc & 255
    mirrored = rest > HALF
    slot = jnp.where(mirrored, 256 - rest, rest)
    column = (loc >> 8) + jnp.where(mirrored, 64, 0)
    return slot, column


def kernel(nr, nc, x_hbm, g_hbm, rows_hbm, cols_hbm, first_hbm, twiddle_hbm, second_hbm, o_ref,
           x_own, g_own, x_in, g_in, rows, cols, first, twiddle, second, spread, packed, z_high, z_low, d_pair,
           pick, picked, part, got,
           load_sem, own_sem, x_send, x_recv, g_send, g_recv, p_send, p_recv, x_ready, g_ready, peers, everyone):
    r, c = lax.axis_index("row"), lax.axis_index("col")
    y, core, z, x = r >> 1, r & 1, c >> 2, c & 3
    locs = rows.shape[1]

    own = [pltpu.make_async_copy(g_hbm, g_own, own_sem.at[0]), pltpu.make_async_copy(x_hbm, x_own, own_sem.at[1])]
    for load in own:
        load.start()

    def row_place(row):
        at = row >> 1
        return (8 * ((at + 3) >> 2) - ((at + 1) >> 2) - 3 * (row & 1)) * nr * nc + row

    def col_place(col):
        plane, at = col >> 2, col & 3
        late = 9 * ((plane + 3) >> 2) + 3 * (plane >> 1) + ((plane + 1) >> 2) + at + ((at + 1) >> 2)
        return late * nr * nc + col * nr

    def place_of(device):
        return row_place(device[0]) + col_place(device[1])

    place = place_of((r, c))

    x_row = 2 * z + (x >> 1)
    my_g = 2 * ((y - z + 4) & 3) + core
    my_x = nr * (x & 1) + my_g

    def x_dest(j):
        return 2 * ((y + (j >> 1)) & 3) + (j & 1), 4 * y + 2 * core + (j >> 3)

    def g_dest(s):
        return 2 * ((z + (s >> 1)) & 3) + (s & 1), c

    def signal(sem, device):
        pl.semaphore_signal(sem, inc=1, device_id=device, device_id_type=MESH)

    barrier = pltpu.get_barrier_semaphore()
    partners = [x_dest(j) for j in range(nc)] + [(x_row, j) for j in range(nc)] + [(r, j) for j in range(nc)]
    partners += [(s, c) for s in range(nr)]
    count = 0
    for device in partners:
        there = place_of(device)

        @pl.when(there > place)
        def _():
            signal(barrier, device)

        count = count + (there < place).astype(jnp.int32)

    loads = [(rows_hbm, rows), (cols_hbm, cols), (first_hbm, first), (twiddle_hbm, twiddle), (second_hbm, second)]
    loads = [pltpu.make_async_copy(a, b, load_sem.at[i]) for i, (a, b) in enumerate(loads)]
    for load in loads:
        load.start()

    def wait_for(sem, number):
        @pl.when(number > 0)
        def _():
            pl.semaphore_wait(sem, number)

    wait_for(barrier, count)

    def tell_earlier(sem, device):
        @pl.when(place_of(device) < place)
        def _():
            signal(sem, device)

    def g_copy(i):
        s = (r + i) & (nr - 1)
        return s, g_dest(s), g_own.at[s], g_in.at[r], g_send, g_recv.at[y]

    def x_copy(i):
        j = (c - i) & (nc - 1)
        return j, x_dest(j), x_own.at[j], x_in.at[c], x_send, x_recv.at[z]

    def remote(device, src, dst, send_sem, recv_sem):
        return pltpu.make_async_remote_copy(
            src_ref=src, dst_ref=dst, send_sem=send_sem, recv_sem=recv_sem,
            device_id=device, device_id_type=MESH)

    def send_early(copy):
        _, device, src, dst, _, recv_sem = copy

        @pl.when(place_of(device) < place)
        def _():
            remote(*copy[1:]).start()

        @pl.when(place_of(device) == place)
        def _():
            pltpu.make_async_copy(src, dst, recv_sem).start()

    def send_late(copy, ready):
        group, device = copy[:2]

        @pl.when(place_of(device) > place)
        def _():
            pl.semaphore_wait(ready.at[group], 1)
            remote(*copy[1:]).start()

    for s in range(nr):
        tell_earlier(g_ready.at[my_g], (s, c))
    for j in range(nc):
        tell_earlier(x_ready.at[my_x], (x_row, j))
    own[0].wait()
    for i in range(nr):
        send_early(g_copy(i))
    own[1].wait()
    for i in range(nc):
        send_early(x_copy(i))
    for j in range(nc):
        tell_earlier(peers, (r, j))
    for i in range(nr):
        send_late(g_copy(i), g_ready)
    for i in range(nc):
        send_late(x_copy(i), x_ready)

    for load in loads:
        load.wait()

    for side, loc_ref in ((0, rows), (1, cols)):
        _, column = digits(loc_ref[...])
        lane = lax.broadcasted_iota(jnp.int32, (HALF, locs), 0)
        hot = (lane == column).astype(F32).astype(BF16)
        pick[side, :HALF, :] = hot
        pick[side, HALF:, :] = hot

    def spectrum(side, arrived, recv_sem, loc_ref):
        sources, _, width = arrived.shape
        steps = width // HALF
        for s in range(sources):
            if s % (sources // 4) == 0:
                some = arrived.at[pl.ds(s, sources // 4)]
                pltpu.make_async_copy(some, some, recv_sem.at[4 * s // sources]).wait()
            block = arrived[s].astype(F32)
            for k in range(steps):
                spread[pl.ds((s * steps + k) * TOK, TOK), :] = block[:, k * HALF:(k + 1) * HALF]
        for t in range(TOK):
            column = spread[pl.ds(t, HALF, stride=TOK), :].astype(BF16)
            packed[:HALF, t * HALF:(t + 1) * HALF] = column
            packed[HALF:, t * HALF:(t + 1) * HALF] = column
        tc, ts = twiddle[0], twiddle[1]
        for t in range(TOK):
            if t % 2 == 0:
                both = jnp.dot(first[...], packed[:, t * HALF:(t + 2) * HALF], preferred_element_type=F32)
            y = both[:, (t % 2) * HALF:(t % 2 + 1) * HALF]
            yc, ys = y[:FP], y[FP:]
            for part_at, z in ((0, yc * tc - ys * ts), (HALF, yc * ts + ys * tc)):
                high = z.astype(BF16)
                z_high[t * FP:(t + 1) * FP, part_at:part_at + HALF] = high
                z_low[t * FP:(t + 1) * FP, part_at:part_at + HALF] = (z - high.astype(F32)).astype(BF16)
        wide = jnp.dot(z_high[...], second[...], preferred_element_type=F32)
        d = wide[:, :HALF] + wide[:, HALF:] + jnp.dot(z_low[...], second[:, :HALF], preferred_element_type=F32)
        high = d.astype(BF16)
        d_pair[:, :HALF] = high
        d_pair[:, HALF:] = (d - high.astype(F32)).astype(BF16)
        tile, group = 256, TOK // 2
        for k in range(locs // tile):
            at = slice(k * tile, (k + 1) * tile)
            slot, _ = digits(loc_ref[:, at])
            mask = lax.broadcasted_iota(jnp.int32, (FP, tile), 0) == slot
            for start in range(0, TOK, group):
                lines = d_pair[start * FP:(start + group) * FP, :]
                found = jnp.dot(lines, pick[side, :, at], preferred_element_type=F32)
                for t in range(group):
                    mine = jnp.where(mask, found[t * FP:(t + 1) * FP], 0.0)
                    picked[side, start + t:start + t + 1, at] = jnp.sum(mine, axis=0, keepdims=True)

    wait_for(peers, sum((place_of((r, j)) > place).astype(jnp.int32) for j in range(nc)))
    for i in range(1, nr):
        signal(everyone, ((r + i) & (nr - 1), c))

    spectrum(0, g_in, g_recv, rows)

    spectrum(1, x_in, x_recv, cols)

    def norming(loc_ref):
        return jnp.where(loc_ref[...] == 0, math.sqrt(1.0 / N), math.sqrt(2.0 / N))

    total = jnp.sum(picked[0] * picked[1], axis=0, keepdims=True) * (norming(rows) * norming(cols))
    width = locs // nc
    for k in range(nc):
        part[k] = total[:, k * width:(k + 1) * width]

    pl.semaphore_wait(everyone, nr - 1)
    mine = c + nc * r
    pltpu.make_async_copy(part.at[c], got.at[mine], p_recv).start()
    for k in range(nc):
        for i in range(nr):
            if i + k:
                row, col = (r + i) & (nr - 1), (c + k) & (nc - 1)
                remote((row, col), part.at[col], got.at[mine], p_send, p_recv).start()
    pltpu.make_async_copy(got, got, p_recv).wait()
    o_ref[...] = jnp.sum(got[...], axis=0)

    sent = got.at[pl.ds(0, nr * nc - 1)]
    pltpu.make_async_copy(sent, sent, p_send).wait()

    def all_sent(copies, source, sem):
        n = source.shape[0]
        stays = [(place_of(device) == place).astype(jnp.int32) for _, device, *_ in copies]
        stays = sum(stays[1:], stays[0])
        for left in (0, 1):
            @pl.when(stays == left)
            def _():
                moved = source.at[pl.ds(0, n - left)]
                pltpu.make_async_copy(moved, moved, sem).wait()

    all_sent([g_copy(i) for i in range(nr)], g_own, g_send)
    all_sent([x_copy(i) for i in range(nc)], x_own, x_send)


def solution(mesh):
    nr, nc = mesh.shape["row"], mesh.shape["col"]
    first, twiddle, second = tables()

    def local(tokens_in, out_grads, loc_rows, loc_cols):
        locs = loc_rows.shape[0]
        x = tokens_in.reshape(nc, TOK, tokens_in.shape[1])
        g = out_grads.reshape(nr, TOK, out_grads.shape[1])
        width = locs // nc
        dma, regular = pltpu.SemaphoreType.DMA, pltpu.SemaphoreType.REGULAR
        out = pl.pallas_call(
            lambda *refs: kernel(nr, nc, *refs),
            out_shape=jax.ShapeDtypeStruct((1, width), F32),
            in_specs=[pl.BlockSpec(memory_space=pl.ANY)] * 7,
            out_specs=pl.BlockSpec(memory_space=pltpu.VMEM),
            scratch_shapes=[
                pltpu.VMEM(x.shape, BF16),
                pltpu.VMEM(g.shape, BF16),
                pltpu.VMEM((nc, TOK, x.shape[2]), BF16),
                pltpu.VMEM((nr, TOK, g.shape[2]), BF16),
                pltpu.VMEM((1, locs), jnp.int32),
                pltpu.VMEM((1, locs), jnp.int32),
                pltpu.VMEM(first.shape, BF16),
                pltpu.VMEM(twiddle.shape, F32),
                pltpu.VMEM(second.shape, BF16),
                pltpu.VMEM((HALF * TOK, HALF), F32),
                pltpu.VMEM((2 * HALF, TOK * HALF), BF16),
                pltpu.VMEM((TOK * FP, 2 * HALF), BF16),
                pltpu.VMEM((TOK * FP, 2 * HALF), BF16),
                pltpu.VMEM((TOK * FP, 2 * HALF), BF16),
                pltpu.VMEM((2, 2 * HALF, locs), BF16),
                pltpu.VMEM((2, TOK, locs), F32),
                pltpu.VMEM((nc, 1, width), F32),
                pltpu.VMEM((nr * nc, 1, width), F32),
                dma((5,)), dma((2,)), dma, dma((4,)), dma, dma((4,)), dma, dma,
                regular((nc,)), regular((nr,)), regular, regular,
            ],
            compiler_params=pltpu.CompilerParams(collective_id=0, has_side_effects=True),
            name="spectral",
        )(x, g, loc_rows.reshape(1, locs), loc_cols.reshape(1, locs),
          jnp.asarray(first), jnp.asarray(twiddle), jnp.asarray(second))
        return out.reshape(width)

    in_specs = (P("row", "col"), P("col", "row"), P(), P())
    return jax.shard_map(local, mesh=mesh, in_specs=in_specs, out_specs=P("col"), check_vma=False)
```
